512 devices in a mesh: wide: 64 (over y, z_hi, core), batch: 8 (over z_lo, x).
Axes of the slice: x: 4, y: 8, z: 8 (z_hi: 4, z_lo: 2; z = z_hi * 2 + z_lo), core: 2. Of those that a mesh axis runs over, the one named last changes fastest.
Arguments:
- integrals: bfloat16 [1536, 64, 640], P('wide'), may hold values from -0.8984375 to 0.8984375
- vir_coeff: bfloat16 [640, 512], P(None, 'batch'), may hold values from -0.25 to 0.25
- occ_energy: float32 [64], replicated, may hold values from -1.6 to -0.4
- vir_energy: float32 [512], replicated, may hold values from 0.2 to 3
- kappas: float32 [8], replicated, may hold values from 0.1 to 3
Outputs:
- density: bfloat16 [8, 64, 512, 1536], P(None, 'wide', 'batch')
The draws below stay inside these ranges and needn't reach their ends.
All inputs are finite; a program needn't handle non-finite values.
Results may differ from the reference program's by a relative error of at most 0.0051.
Values may be sent and summed in bfloat16 or wider, within the bound.
A program may use at most 64 MiB of HBM per device.

```python
import math
import jax
import jax.numpy as jnp
from jax import lax

NBF = 640
NAUX = 1536
NVIR = 512
NKAP = 8
HALF = 2
NOCC = 64


def steps_of(stream_key, dims, split, low, largest):
    gain, own = 1.0, jax.random.fold_in(stream_key, 6)
    for position, parts in split:
        draws = jnp.exp(jax.random.uniform(jax.random.fold_in(own, position), (parts,), jnp.float32, low / len(split), largest / len(split)))
        gain = gain * jnp.repeat(draws, dims[position] // parts).reshape([-1 if axis == position else 1 for axis in range(len(dims))])
    return gain


def scatter_about(key, extent, deviation, bound, cuts=(), held_as=jnp.bfloat16):
    values = deviation * jax.random.normal(key, extent, jnp.float32)
    if cuts:
        values = values * steps_of(key, extent, cuts, -0.22, 0.18)
    return jnp.clip(values, -bound, bound).astype(held_as)


def setup_inputs(seed: int = 0) -> dict:
    keys = jax.random.split(jax.random.key(seed), 6)
    integrals = scatter_about(keys[0], (NAUX, NOCC, NBF), 0.15, 0.8984375, ((0, 64),))
    vir_coeff = scatter_about(keys[1], (NBF, NVIR), NBF ** -0.5, 0.25, ((1, 8),))
    occ_energy = jnp.clip(jax.random.uniform(keys[2], (NOCC,), jnp.float32, -1.6, -0.4), -1.6, -0.4)
    vir_energy = jnp.clip(jax.random.uniform(keys[3], (NVIR,), jnp.float32, 0.2, 3.0), 0.2, 3.0)
    kappas = jnp.clip(jnp.exp(jax.random.uniform(keys[4], (NKAP,), jnp.float32, math.log(0.1), math.log(3.0))), 0.1, 3.0)
    return dict(integrals=integrals, vir_coeff=vir_coeff, occ_energy=occ_energy, vir_energy=vir_energy, kappas=kappas)


def pair_density(own, partner, own_energy, partner_energy, row_energy, vir_energy, kappas):
    coulomb = jnp.dot(own.T, partner, preferred_element_type=jnp.float32)
    denominator = row_energy[:, None] + vir_energy[None, :] - own_energy - partner_energy
    damping = 1.0 - jnp.exp(-kappas[:, None, None] * denominator[None])
    amplitude = ((-coulomb[None] * (damping * damping)) / denominator[None]).astype(jnp.bfloat16)
    return jnp.einsum("kab,pb->kap", amplitude.astype(jnp.float32), partner.astype(jnp.float32))


def reference(integrals, vir_coeff, occ_energy, vir_energy, kappas):
    flat = integrals.reshape(NAUX * NOCC, NBF)
    transformed = jnp.dot(flat, vir_coeff, preferred_element_type=jnp.float32).astype(jnp.bfloat16)
    by_occ = jnp.transpose(transformed.reshape(NAUX, NOCC, NVIR), (1, 0, 2))

    def one_orbital(index):
        own = by_occ[index]
        density = jnp.zeros((NKAP, NVIR, NAUX), jnp.float32)
        for offset in range(-HALF, HALF + 1):
            other = ((index + offset) % NOCC).astype(jnp.int32)
            density = density + pair_density(own, by_occ[other], occ_energy[index], occ_energy[other], vir_energy, vir_energy, kappas)
        return density.astype(jnp.bfloat16)

    result = lax.map(one_orbital, jnp.arange(NOCC, dtype=jnp.int32))
    return jnp.transpose(result, (1, 0, 2, 3))
```

```python
import functools

import jax
import jax.numpy as jnp
from jax import lax
from jax.experimental import pallas as pl
from jax.experimental.pallas import tpu as pltpu
from jax.sharding import PartitionSpec as P

HALF = 2
NX = 4
MESH = pl.DeviceIdType.MESH
ORDER = (1, 0, 2)


def kernel(
    ny, nz, ints_ref, coef_ref, vir_ref, occ_ref, kap_ref, out_ref,
    full, mine, rows, gath, tit, row_exp, vir2, kvec, row_e, amp, acc,
    local_sem, y_send, y_recv, z_send, z_recv, g_send, g_recv, s_send, s_recv,
):
    wide = lax.axis_index("wide")
    batch = lax.axis_index("batch")
    core = lax.rem(wide, 2)
    zh = lax.rem(wide // 2, nz)
    y = wide // (2 * nz)
    x = lax.rem(batch, NX)
    zl = batch // NX
    pairs = ny * nz
    own_pair = wide // 2
    naux = out_ref.shape[1]

    def at_wide(yy, zz, cc):
        return {"wide": (yy * nz + zz) * 2 + cc, "batch": batch}

    def at_batch(dx, dz):
        return lax.rem(zl + dz, 2) * NX + lax.rem(x + dx + NX, NX)

    def dev_batch(dx, dz):
        return {"wide": wide, "batch": at_batch(dx, dz)}

    sibling = at_wide(y, zh, 1 - core)
    left, right, over = dev_batch(-1, 0), dev_batch(1, 0), dev_batch(0, 1)

    barrier = pltpu.get_barrier_semaphore()
    peers = [at_wide(lax.rem(y + d, ny), zh, core) for d in range(1, ny)]
    peers += [at_wide(y, lax.rem(zh + d, nz), core) for d in range(1, nz)]
    peers += [left, right, over, sibling]
    for peer in peers:
        pl.semaphore_signal(barrier, inc=1, device_id=peer, device_id_type=MESH)

    coef2 = jnp.concatenate([coef_ref[...], coef_ref[...]], axis=1)
    steps = 4
    tall = full.shape[0] // steps

    def transform(s, carry):
        at = pl.multiple_of(s * tall, tall)
        full[pl.ds(at, tall), :] = jnp.dot(
            ints_ref[pl.ds(at, tall), :], coef2, preferred_element_type=jnp.float32
        )
        return carry

    lax.fori_loop(0, steps, transform, 0)
    nocc = 2 * pairs
    nrow = full.shape[0] // nocc
    low = lax.broadcasted_iota(jnp.int32, (nrow, 128), 1) < 64
    for m in range(pairs):
        even = full[pl.ds(2 * m, nrow, stride=nocc), :]
        odd = full[pl.ds(2 * m + 1, nrow, stride=nocc), :]
        tile = jnp.where(low, even, odd).reshape(nrow // 8, 8, 128).astype(jnp.bfloat16)
        mine[m + 1] = tile
        if m == 0:
            mine[pairs + 1] = tile
        if m == pairs - 1:
            mine[0] = tile

    pl.semaphore_wait(barrier, len(peers))

    def y_copy(yy, src_y):
        return pltpu.make_async_remote_copy(
            src_ref=mine.at[pl.ds(nz * yy, nz + 2)],
            dst_ref=rows.at[:, src_y],
            send_sem=y_send.at[yy],
            recv_sem=y_recv.at[src_y],
            device_id=at_wide(yy, zh, core),
            device_id_type=MESH,
        )

    far_first = sorted(range(1, ny), key=lambda d: -min(d, ny - d))
    for d in far_first:
        y_copy(lax.rem(y + d, ny), y).start()
    y_own = pltpu.make_async_copy(mine.at[pl.ds(nz * y, nz + 2)], rows.at[:, y], local_sem.at[0])
    y_own.start()

    for b in range(2 * NX):
        part = vir_ref[:, b * 64 : (b + 1) * 64]
        vir2[pl.ds(b, 1), :] = jnp.concatenate([part, part], axis=1)
    qs = lax.broadcasted_iota(jnp.int32, (8, 128), 0)
    kv = jnp.zeros((8, 128), jnp.float32)
    for q in range(8):
        kv = jnp.where(qs == q, kap_ref[q], kv)
    kvec[...] = kv
    columns = jnp.transpose(vir2[...])
    pick = lax.broadcasted_iota(jnp.int32, (128, 8), 1) == batch
    row_energy = jnp.sum(jnp.where(pick, columns, 0.0), axis=1, keepdims=True)[:64]
    row_energy = jnp.broadcast_to(row_energy - occ_ref[wide], (64, 128))
    row_e[...] = row_energy
    for q in range(8):
        row_exp[pl.ds(q * 64, 64), :] = jnp.exp(-kap_ref[q] * row_energy)

    y_own.wait()
    for d in range(1, ny):
        src_y = lax.rem(y + d, ny)
        y_copy(src_y, src_y).wait_recv()

    def z_copy(p, zz, src_z):
        return pltpu.make_async_remote_copy(
            src_ref=rows.at[zz + p],
            dst_ref=gath.at[batch, p, :, src_z, core],
            send_sem=z_send.at[p, zz],
            recv_sem=z_recv.at[p, src_z],
            device_id=at_wide(y, zz, core),
            device_id_type=MESH,
        )

    z_far_first = sorted(range(1, nz), key=lambda d: -min(d, nz - d))
    z_own = {}
    for p in ORDER:
        for d in z_far_first:
            z_copy(p, lax.rem(zh + d, nz), zh).start()
        z_own[p] = pltpu.make_async_copy(
            rows.at[zh + p], gath.at[batch, p, :, zh, core], local_sem.at[1 + p]
        )
        z_own[p].start()

    half = ny // 2
    parts = {"all": pl.ds(0, ny), "first": pl.ds(0, half), "second": pl.ds(half, ny - half)}

    def g_copy(p, dx, dz, part, slot, to):
        ref = gath.at[at_batch(dx, dz), p, parts[part], :, core]
        return pltpu.make_async_remote_copy(
            src_ref=ref, dst_ref=ref, send_sem=g_send.at[p, slot], recv_sem=g_recv.at[p, slot],
            device_id=to, device_id_type=MESH,
        )

    sends = {
        0: (right, 0, 0, "all"),
        1: (left, 0, 0, "all"),
        2: (over, 0, 0, "all"),
        3: (right, -1, 0, "first"),
        4: (left, 1, 0, "second"),
        5: (right, 0, 1, "all"),
        6: (left, 0, 1, "all"),
        7: (over, 2, 0, "all"),
    }
    gets = {
        0: (-1, 0, "all"),
        1: (1, 0, "all"),
        2: (0, 1, "all"),
        3: (2, 0, "first"),
        4: (2, 0, "second"),
        5: (-1, 1, "all"),
        6: (1, 1, "all"),
        7: (2, 1, "all"),
    }
    blocks = ((0, 0), (-1, 0), (1, 0), (0, 1), (2, 0), (-1, 1), (1, 1), (2, 1))

    def g_start(p, slot):
        to, dx, dz, part = sends[slot]
        g_copy(p, dx, dz, part, slot, to).start()

    def g_wait(p, slot):
        dx, dz, part = gets[slot]
        g_copy(p, dx, dz, part, slot, right).wait_recv()

    def s_copy(p, block, cc):
        dx, dz = blocks[block]
        ref = gath.at[at_batch(dx, dz), p, :, :, cc]
        return pltpu.make_async_remote_copy(
            src_ref=ref, dst_ref=ref, send_sem=s_send.at[p, block], recv_sem=s_recv.at[p, block],
            device_id=sibling, device_id_type=MESH,
        )

    def s_start(p, block):
        s_copy(p, block, core).start()

    def s_wait(p, block):
        s_copy(p, block, 1 - core).wait_recv()

    def flat(b, p):
        return gath.at[b, p].reshape(naux, 128)

    lane = lax.broadcasted_iota(jnp.int32, (1, 128), 1)
    lane_low = lane < 64
    tn = 256 if naux % 256 == 0 else naux

    def compute(p, first_block, second_block, first, last):
        b0 = at_batch(*blocks[first_block])
        b1 = at_batch(*blocks[second_block])
        r0, r1 = flat(b0, p), flat(b1, p)
        pair = lax.rem(own_pair + p - 1 + pairs, pairs)
        occ_j = jnp.where(lane_low, occ_ref[2 * pair], occ_ref[2 * pair + 1])
        offset = 2 * (p - 1) + jnp.where(lane_low, 0, 1) - core
        keep = jnp.logical_and(offset >= -HALF, offset <= HALF)
        for n, (b, r) in enumerate(((b0, r0), (b1, r1))):
            coulomb = jnp.dot(
                tit[pl.ds(pl.multiple_of(core * 64, 64), 64), :], r[...],
                preferred_element_type=jnp.float32,
            )
            col_e = vir2[pl.ds(b, 1), :] - occ_j
            scaled = -coulomb / (row_e[...] + col_e)
            scaled = jnp.where(keep, scaled, 0.0)
            col_exp = jnp.exp(-kvec[...] * col_e)
            for q in range(8):
                damp = 1.0 - row_exp[pl.ds(q * 64, 64), :] * col_exp[q : q + 1, :]
                amp[pl.ds(q * 64, 64), n * 128 : (n + 1) * 128] = (scaled * (damp * damp)).astype(
                    jnp.bfloat16
                )

        def tile(n, carry):
            at = pl.multiple_of(n * tn, tn)
            rhs = jnp.concatenate([r0[pl.ds(at, tn), :], r1[pl.ds(at, tn), :]], axis=1)
            part = lax.dot_general(
                amp[...], rhs, (((1,), (1,)), ((), ())), preferred_element_type=jnp.float32
            )
            if first:
                acc[:, pl.ds(at, tn)] = part
            elif last:
                out_ref[:, pl.ds(at, tn)] = (acc[:, pl.ds(at, tn)] + part).astype(jnp.bfloat16)
            else:
                acc[:, pl.ds(at, tn)] += part
            return carry

        lax.fori_loop(0, naux // tn, tile, 0)

    for p in ORDER:
        z_own[p].wait()
        for d in range(1, nz):
            src_z = lax.rem(zh + d, nz)
            z_copy(p, src_z, src_z).wait_recv()
        for slot in (0, 1, 2):
            g_start(p, slot)
        s_start(p, 0)

    for p in ORDER:
        g_wait(p, 0)
        g_start(p, 3)
        s_start(p, 1)
        g_wait(p, 1)
        g_start(p, 4)
        s_start(p, 2)
        g_wait(p, 2)
        g_start(p, 5)
        g_start(p, 6)
        s_start(p, 3)
        for block in range(4):
            s_wait(p, block)
        if p == ORDER[0]:
            tit[...] = jnp.transpose(flat(batch, 1)[...])
        compute(p, 0, 3, p == ORDER[0], False)
        compute(p, 1, 2, False, False)
    for p in ORDER:
        g_wait(p, 3)
        g_wait(p, 4)
        g_start(p, 7)
        s_start(p, 4)
        g_wait(p, 5)
        s_start(p, 5)
        g_wait(p, 6)
        s_start(p, 6)
        g_wait(p, 7)
        s_start(p, 7)
        for block in range(4, 8):
            s_wait(p, block)
        compute(p, 4, 7, False, False)
        compute(p, 5, 6, False, p == ORDER[2])

    for d in range(1, ny):
        y_copy(lax.rem(y + d, ny), y).wait_send()
    for p in range(3):
        for d in range(1, nz):
            z_copy(p, lax.rem(zh + d, nz), zh).wait_send()
        for slot in range(8):
            to, dx, dz, part = sends[slot]
            g_copy(p, dx, dz, part, slot, to).wait_send()
        for block in range(8):
            s_copy(p, block, core).wait_send()


def on_device(ny, nz, integrals, vir_coeff, occ_energy, vir_energy, kappas):
    aux_local, nocc, basis = integrals.shape
    naux = aux_local * ny * nz * 2
    pairs = ny * nz
    vmem = pl.BlockSpec(memory_space=pltpu.VMEM)
    smem = pl.BlockSpec(memory_space=pltpu.SMEM)
    sub = aux_local // 8
    bf16, f32 = jnp.bfloat16, jnp.float32
    dma = pltpu.SemaphoreType.DMA
    out = pl.pallas_call(
        functools.partial(kernel, ny, nz),
        out_shape=jax.ShapeDtypeStruct((8 * 64, naux), bf16),
        in_specs=[vmem, vmem, vmem, smem, smem],
        out_specs=vmem,
        scratch_shapes=[
            pltpu.VMEM((aux_local * nocc, 128), f32),
            pltpu.VMEM((pairs + 2, sub, 8, 128), bf16),
            pltpu.VMEM((nz + 2, ny, sub, 8, 128), bf16),
            pltpu.VMEM((2 * NX, 3, ny, nz, 2, sub, 8, 128), bf16),
            pltpu.VMEM((128, naux), bf16),
            pltpu.VMEM((512, 128), f32),
            pltpu.VMEM((8, 128), f32),
            pltpu.VMEM((8, 128), f32),
            pltpu.VMEM((64, 128), f32),
            pltpu.VMEM((512, 256), bf16),
            pltpu.VMEM((512, naux), f32),
            dma((4,)),
            dma((ny,)),
            dma((ny,)),
            dma((3, nz)),
            dma((3, nz)),
            dma((3, 8)),
            dma((3, 8)),
            dma((3, 8)),
            dma((3, 8)),
        ],
        compiler_params=pltpu.CompilerParams(
            collective_id=0, has_side_effects=True, vmem_limit_bytes=60 * 1024 * 1024
        ),
    )(
        integrals.reshape(aux_local * nocc, basis), vir_coeff, vir_energy.reshape(1, -1),
        occ_energy, kappas,
    )
    return out.reshape(8, 1, 64, naux)


def solution(mesh):
    wide = mesh.shape["wide"]
    nz = 4 if wide == 64 else 2
    ny = wide // (2 * nz)
    return jax.shard_map(
        functools.partial(on_device, ny, nz),
        mesh=mesh,
        in_specs=(P("wide", None, None), P(None, "batch"), P(), P(), P()),
        out_specs=P(None, "wide", "batch", None),
        check_vma=False,
    )
```

```python
import functools

import jax
import jax.numpy as jnp
from jax import lax
from jax.experimental import pallas as pl
from jax.experimental.pallas import tpu as pltpu
from jax.sharding import PartitionSpec as P

HALF = 2
NX = 4
MESH = pl.DeviceIdType.MESH


def kernel(
    ny, nz, ints_ref, coef_ref, vir_ref, occ_ref, kap_ref, out_ref,
    ints, full, mine, rows, gath, tit, row_exp, vir2, kvec, row_e, amp, acc,
    in_sem, local_sem, y_send, y_recv, z_send, z_recv, g_send, g_recv, s_send, s_recv,
):
    wide = lax.axis_index("wide")
    batch = lax.axis_index("batch")
    core = lax.rem(wide, 2)
    zh = lax.rem(wide // 2, nz)
    y = wide // (2 * nz)
    x = lax.rem(batch, NX)
    zl = batch // NX
    pairs = ny * nz
    own_pair = wide // 2
    naux = out_ref.shape[1]

    def at_wide(yy, zz, cc):
        return {"wide": (yy * nz + zz) * 2 + cc, "batch": batch}

    def at_batch(dx, dz):
        return lax.rem(zl + dz, 2) * NX + lax.rem(x + dx + NX, NX)

    def dev_batch(dx, dz):
        return {"wide": wide, "batch": at_batch(dx, dz)}

    sibling = at_wide(y, zh, 1 - core)
    left, right, over = dev_batch(-1, 0), dev_batch(1, 0), dev_batch(0, 1)

    steps = in_sem.shape[0]
    tall = full.shape[0] // steps

    def fetch(k):
        part = pl.ds(k * tall, tall)
        return pltpu.make_async_copy(ints_ref.at[part], ints.at[part], in_sem.at[k])

    for k in range(steps):
        fetch(k).start()

    barrier = pltpu.get_barrier_semaphore()
    peers = [at_wide(lax.rem(y + d, ny), zh, core) for d in range(1, ny)]
    peers += [at_wide(y, lax.rem(zh + d, nz), core) for d in range(1, nz)]
    peers += [left, right, over, sibling]
    for peer in peers:
        pl.semaphore_signal(barrier, inc=1, device_id=peer, device_id_type=MESH)

    coef2 = jnp.concatenate([coef_ref[...], coef_ref[...]], axis=0)
    for k in range(steps):
        fetch(k).wait()
        full[pl.ds(k * tall, tall), :] = lax.dot_general(
            ints[pl.ds(k * tall, tall), :], coef2, (((1,), (1,)), ((), ())),
            preferred_element_type=jnp.float32,
        )
    nocc = 2 * pairs
    nrow = full.shape[0] // nocc
    low = lax.broadcasted_iota(jnp.int32, (nrow, 128), 1) < 64
    for m in range(pairs):
        even = full[pl.ds(2 * m, nrow, stride=nocc), :]
        odd = full[pl.ds(2 * m + 1, nrow, stride=nocc), :]
        tile = jnp.where(low, even, odd).reshape(nrow // 8, 8, 128).astype(jnp.bfloat16)
        mine[m + 1] = tile
        if m == 0:
            mine[pairs + 1] = tile
        if m == pairs - 1:
            mine[0] = tile

    pl.semaphore_wait(barrier, len(peers))

    y_parts = ((1, nz), (0, 1), (nz + 1, 1))

    def y_copy(part, yy, src_y):
        at, count = y_parts[part]
        return pltpu.make_async_remote_copy(
            src_ref=mine.at[pl.ds(nz * yy + at, count)],
            dst_ref=rows.at[pl.ds(at, count), src_y],
            send_sem=y_send.at[part, yy],
            recv_sem=y_recv.at[part, src_y],
            device_id=at_wide(yy, zh, core),
            device_id_type=MESH,
        )

    far_first = sorted(range(1, ny), key=lambda d: -min(d, ny - d))
    for part in range(3):
        for d in far_first:
            y_copy(part, lax.rem(y + d, ny), y).start()
    y_own = pltpu.make_async_copy(mine.at[pl.ds(nz * y, nz + 2)], rows.at[:, y], local_sem.at[0])
    y_own.start()

    for b in range(2 * NX):
        part = vir_ref[:, b * 64 : (b + 1) * 64]
        vir2[pl.ds(b, 1), :] = jnp.concatenate([part, part], axis=1)
    qs = lax.broadcasted_iota(jnp.int32, (8, 128), 0)
    kv = jnp.zeros((8, 128), jnp.float32)
    for q in range(8):
        kv = jnp.where(qs == q, kap_ref[q], kv)
    kvec[...] = kv
    columns = jnp.transpose(vir2[...])
    pick = lax.broadcasted_iota(jnp.int32, (128, 8), 1) == batch
    row_energy = jnp.sum(jnp.where(pick, columns, 0.0), axis=1, keepdims=True)[:64]
    row_energy = jnp.broadcast_to(row_energy - occ_ref[wide], (64, 128))
    row_e[...] = row_energy
    for q in range(8):
        row_exp[pl.ds(q * 64, 64), :] = jnp.exp(-kap_ref[q] * row_energy)

    y_own.wait()

    def y_wait(part):
        for d in range(1, ny):
            src_y = lax.rem(y + d, ny)
            y_copy(part, src_y, src_y).wait_recv()

    def z_copy(p, zz, src_z):
        return pltpu.make_async_remote_copy(
            src_ref=rows.at[zz + p],
            dst_ref=gath.at[batch, p, :, src_z, core],
            send_sem=z_send.at[p, zz],
            recv_sem=z_recv.at[p, src_z],
            device_id=at_wide(y, zz, core),
            device_id_type=MESH,
        )

    z_far_first = sorted(range(1, nz), key=lambda d: -min(d, nz - d))

    def z_own(p):
        return pltpu.make_async_copy(
            rows.at[zh + p], gath.at[batch, p, :, zh, core], local_sem.at[1 + p]
        )

    def z_start(p):
        for d in z_far_first:
            z_copy(p, lax.rem(zh + d, nz), zh).start()
        z_own(p).start()

    def z_wait(p):
        z_own(p).wait()
        for d in range(1, nz):
            src_z = lax.rem(zh + d, nz)
            z_copy(p, src_z, src_z).wait_recv()

    half = ny // 2
    parts = {"all": pl.ds(0, ny), "first": pl.ds(0, half), "second": pl.ds(half, ny - half)}

    def g_copy(p, dx, dz, part, slot, to):
        ref = gath.at[at_batch(dx, dz), p, parts[part], :, core]
        return pltpu.make_async_remote_copy(
            src_ref=ref, dst_ref=ref, send_sem=g_send.at[p, slot], recv_sem=g_recv.at[p, slot],
            device_id=to, device_id_type=MESH,
        )

    sends = {
        0: (right, 0, 0, "all"),
        1: (left, 0, 0, "all"),
        2: (over, 0, 0, "all"),
        3: (right, -1, 0, "first"),
        4: (left, 1, 0, "second"),
        5: (right, 0, 1, "all"),
        6: (left, 0, 1, "all"),
        7: (over, 2, 0, "all"),
    }
    gets = {
        0: (-1, 0, "all"),
        1: (1, 0, "all"),
        2: (0, 1, "all"),
        3: (2, 0, "first"),
        4: (2, 0, "second"),
        5: (-1, 1, "all"),
        6: (1, 1, "all"),
        7: (2, 1, "all"),
    }
    blocks = ((0, 0), (-1, 0), (1, 0), (0, 1), (2, 0), (-1, 1), (1, 1), (2, 1))

    def g_start(p, slot):
        to, dx, dz, part = sends[slot]
        g_copy(p, dx, dz, part, slot, to).start()

    def g_wait(p, slot):
        dx, dz, part = gets[slot]
        g_copy(p, dx, dz, part, slot, right).wait_recv()

    def s_copy(p, block, cc):
        dx, dz = blocks[block]
        ref = gath.at[at_batch(dx, dz), p, :, :, cc]
        return pltpu.make_async_remote_copy(
            src_ref=ref, dst_ref=ref, send_sem=s_send.at[p, block], recv_sem=s_recv.at[p, block],
            device_id=sibling, device_id_type=MESH,
        )

    def s_start(p, block):
        s_copy(p, block, core).start()

    def s_wait(p, block):
        s_copy(p, block, 1 - core).wait_recv()

    def flat(b, p):
        return gath.at[b, p].reshape(naux, 128)

    lane = lax.broadcasted_iota(jnp.int32, (1, 128), 1)
    lane_low = lane < 64
    tn = 256 if naux % 256 == 0 else naux

    def compute(p, first_block, second_block, first, last):
        b0 = at_batch(*blocks[first_block])
        b1 = at_batch(*blocks[second_block])
        r0, r1 = flat(b0, p), flat(b1, p)
        pair = lax.rem(own_pair + p - 1 + pairs, pairs)
        occ_j = jnp.where(lane_low, occ_ref[2 * pair], occ_ref[2 * pair + 1])
        offset = 2 * (p - 1) + jnp.where(lane_low, 0, 1) - core
        keep = jnp.logical_and(offset >= -HALF, offset <= HALF)
        for n, (b, r) in enumerate(((b0, r0), (b1, r1))):
            coulomb = jnp.dot(
                tit[pl.ds(pl.multiple_of(core * 64, 64), 64), :], r[...],
                preferred_element_type=jnp.float32,
            )
            col_e = vir2[pl.ds(b, 1), :] - occ_j
            scaled = -coulomb / (row_e[...] + col_e)
            scaled = jnp.where(keep, scaled, 0.0)
            col_exp = jnp.exp(-kvec[...] * col_e)
            for q in range(8):
                damp = 1.0 - row_exp[pl.ds(q * 64, 64), :] * col_exp[q : q + 1, :]
                amp[pl.ds(q * 64, 64), n * 128 : (n + 1) * 128] = (scaled * (damp * damp)).astype(
                    jnp.bfloat16
                )

        def tile(n, carry):
            at = pl.multiple_of(n * tn, tn)
            rhs = jnp.concatenate([r0[pl.ds(at, tn), :], r1[pl.ds(at, tn), :]], axis=1)
            part = lax.dot_general(
                amp[...], rhs, (((1,), (1,)), ((), ())), preferred_element_type=jnp.float32
            )
            if first:
                acc[:, pl.ds(at, tn)] = part
            elif last:
                out_ref[:, pl.ds(at, tn)] = (acc[:, pl.ds(at, tn)] + part).astype(jnp.bfloat16)
            else:
                acc[:, pl.ds(at, tn)] += part
            return carry

        lax.fori_loop(0, naux // tn, tile, 0)

    def own(p):
        z_wait(p)
        for slot in (0, 1, 2):
            g_start(p, slot)
        s_start(p, 0)

    def near(p):
        g_wait(p, 0)
        g_start(p, 3)
        s_start(p, 1)
        g_wait(p, 1)
        g_start(p, 4)
        s_start(p, 2)
        g_wait(p, 2)
        g_start(p, 5)
        g_start(p, 6)
        s_start(p, 3)

    def opposite(p):
        g_wait(p, 3)
        g_wait(p, 4)
        g_start(p, 7)
        s_start(p, 4)

    def last_of(p):
        for slot, block in ((5, 5), (6, 6), (7, 7)):
            g_wait(p, slot)
            s_start(p, block)

    def shared(p, *which):
        for block in which:
            s_wait(p, block)

    def near_compute(p):
        shared(p, 0, 1, 2, 3)
        if p == 1:
            tit[...] = jnp.transpose(flat(batch, 1)[...])
        compute(p, 0, 3, p == 1, False)
        compute(p, 1, 2, False, False)

    def far_compute(p):
        shared(p, 4, 5, 6, 7)
        compute(p, 5, 6, False, False)
        compute(p, 4, 7, False, p == 2)

    y_wait(0)
    z_start(1)
    y_wait(1)
    y_wait(2)
    z_start(0)
    z_start(2)
    own(1)
    own(0)
    near(1)
    near_compute(1)
    own(2)
    near(0)
    near_compute(0)
    opposite(1)
    near(2)
    near_compute(2)
    opposite(0)
    last_of(1)
    far_compute(1)
    opposite(2)
    last_of(0)
    far_compute(0)
    last_of(2)
    far_compute(2)

    for part in range(3):
        for d in range(1, ny):
            y_copy(part, lax.rem(y + d, ny), y).wait_send()
    for p in range(3):
        for d in range(1, nz):
            z_copy(p, lax.rem(zh + d, nz), zh).wait_send()
        for slot in range(8):
            to, dx, dz, part = sends[slot]
            g_copy(p, dx, dz, part, slot, to).wait_send()
        for block in range(8):
            s_copy(p, block, core).wait_send()


def on_device(ny, nz, integrals, vir_coeff, occ_energy, vir_energy, kappas):
    aux_local, nocc, basis = integrals.shape
    naux = aux_local * ny * nz * 2
    pairs = ny * nz
    vmem = pl.BlockSpec(memory_space=pltpu.VMEM)
    smem = pl.BlockSpec(memory_space=pltpu.SMEM)
    sub = aux_local // 8
    bf16, f32 = jnp.bfloat16, jnp.float32
    dma = pltpu.SemaphoreType.DMA
    out = pl.pallas_call(
        functools.partial(kernel, ny, nz),
        out_shape=pltpu.VMEM((8 * 64, naux), bf16),
        in_specs=[pl.BlockSpec(memory_space=pl.ANY), vmem, vmem, smem, smem],
        out_specs=vmem,
        scratch_shapes=[
            pltpu.VMEM((aux_local * nocc, basis), bf16),
            pltpu.VMEM((aux_local * nocc, 128), f32),
            pltpu.VMEM((pairs + 2, sub, 8, 128), bf16),
            pltpu.VMEM((nz + 2, ny, sub, 8, 128), bf16),
            pltpu.VMEM((2 * NX, 3, ny, nz, 2, sub, 8, 128), bf16),
            pltpu.VMEM((128, naux), bf16),
            pltpu.VMEM((512, 128), f32),
            pltpu.VMEM((8, 128), f32),
            pltpu.VMEM((8, 128), f32),
            pltpu.VMEM((64, 128), f32),
            pltpu.VMEM((512, 256), bf16),
            pltpu.VMEM((512, naux), f32),
            dma((4,)),
            dma((4,)),
            dma((3, ny)),
            dma((3, ny)),
            dma((3, nz)),
            dma((3, nz)),
            dma((3, 8)),
            dma((3, 8)),
            dma((3, 8)),
            dma((3, 8)),
        ],
        compiler_params=pltpu.CompilerParams(
            collective_id=0, has_side_effects=True, vmem_limit_bytes=60 * 1024 * 1024
        ),
    )(
        integrals.reshape(aux_local * nocc, basis), vir_coeff.T, vir_energy.reshape(1, -1),
        occ_energy, kappas,
    )
    return out.reshape(8, 1, 64, naux)


def solution(mesh):
    wide = mesh.shape["wide"]
    nz = 4 if wide == 64 else 2
    ny = wide // (2 * nz)
    return jax.shard_map(
        functools.partial(on_device, ny, nz),
        mesh=mesh,
        in_specs=(P("wide", None, None), P(None, "batch"), P(), P(), P()),
        out_specs=P(None, "wide", "batch", None),
        check_vma=False,
    )
```

```python
import functools

import jax
import jax.numpy as jnp
from jax import lax
from jax.experimental import pallas as pl
from jax.experimental.pallas import tpu as pltpu
from jax.sharding import PartitionSpec as P

HALF = 2
NX = 4
MESH = pl.DeviceIdType.MESH


def kernel(
    ny, nz, ints_ref, coef_ref, vir_ref, occ_ref, kap_ref, out_ref,
    ints, full, mine, gath, tit, row_exp, vir2, kvec, row_e, amp, acc,
    in_sem, a_send, a_recv, g_send, g_recv, s_send, s_recv,
):
    wide = lax.axis_index("wide")
    batch = lax.axis_index("batch")
    core = lax.rem(wide, 2)
    zh = lax.rem(wide // 2, nz)
    y = wide // (2 * nz)
    x = lax.rem(batch, NX)
    zl = batch // NX
    pairs = ny * nz
    own_pair = wide // 2
    naux = out_ref.shape[1]

    def at_wide(yy, zz, cc):
        return {"wide": (yy * nz + zz) * 2 + cc, "batch": batch}

    def at_batch(dx, dz):
        return lax.rem(zl + dz, 2) * NX + lax.rem(x + dx + NX, NX)

    def dev_batch(dx, dz):
        return {"wide": wide, "batch": at_batch(dx, dz)}

    sibling = at_wide(y, zh, 1 - core)
    left, right, over = dev_batch(-1, 0), dev_batch(1, 0), dev_batch(0, 1)

    steps = in_sem.shape[0]
    tall = full.shape[0] // steps

    def fetch(k):
        part = pl.ds(k * tall, tall)
        return pltpu.make_async_copy(ints_ref.at[part], ints.at[part], in_sem.at[k])

    for k in range(steps):
        fetch(k).start()

    barrier = pltpu.get_barrier_semaphore()
    far = sorted(
        ((dy, dz) for dy in range(ny) for dz in range(nz) if (dy, dz) != (0, 0)),
        key=lambda d: -min(d[0], ny - d[0]) - 2 * min(d[1], nz - d[1]),
    )
    owners = [(lax.rem(y + dy, ny), lax.rem(zh + dz, nz)) for dy, dz in far]
    peers = [at_wide(yy, zz, core) for yy, zz in owners]
    peers += [left, right, over, sibling]
    for peer in peers:
        pl.semaphore_signal(barrier, inc=1, device_id=peer, device_id_type=MESH)

    coef2 = jnp.concatenate([coef_ref[...], coef_ref[...]], axis=0)
    for k in range(steps):
        fetch(k).wait()
        full[pl.ds(k * tall, tall), :] = lax.dot_general(
            ints[pl.ds(k * tall, tall), :], coef2, (((1,), (1,)), ((), ())),
            preferred_element_type=jnp.float32,
        )
    nocc = 2 * pairs
    nrow = full.shape[0] // nocc
    low = lax.broadcasted_iota(jnp.int32, (nrow, 128), 1) < 64
    for m in range(pairs):
        even = full[pl.ds(2 * m, nrow, stride=nocc), :]
        odd = full[pl.ds(2 * m + 1, nrow, stride=nocc), :]
        tile = jnp.where(low, even, odd).reshape(nrow // 8, 8, 128).astype(jnp.bfloat16)
        mine[m + 1] = tile
        if m == 0:
            mine[pairs + 1] = tile
        if m == pairs - 1:
            mine[0] = tile

    pl.semaphore_wait(barrier, len(peers))

    def a_copy(p, yy, zz):
        return pltpu.make_async_remote_copy(
            src_ref=mine.at[yy * nz + zz + p],
            dst_ref=gath.at[batch, p, y, zh, core],
            send_sem=a_send.at[p],
            recv_sem=a_recv.at[p],
            device_id=at_wide(yy, zz, core),
            device_id_type=MESH,
        )

    for p in (1, 0, 2):
        pltpu.make_async_copy(
            mine.at[own_pair + p], gath.at[batch, p, y, zh, core], a_recv.at[p]
        ).start()
        for yy, zz in owners:
            a_copy(p, yy, zz).start()

    def a_wait(p):
        ref = gath.at[batch, p, :, :, core]
        pltpu.make_async_copy(ref, ref, a_recv.at[p]).wait()

    for b in range(2 * NX):
        part = vir_ref[:, b * 64 : (b + 1) * 64]
        vir2[pl.ds(b, 1), :] = jnp.concatenate([part, part], axis=1)
    qs = lax.broadcasted_iota(jnp.int32, (8, 128), 0)
    kv = jnp.zeros((8, 128), jnp.float32)
    for q in range(8):
        kv = jnp.where(qs == q, kap_ref[q], kv)
    kvec[...] = kv
    columns = jnp.transpose(vir2[...])
    pick = lax.broadcasted_iota(jnp.int32, (128, 8), 1) == batch
    row_energy = jnp.sum(jnp.where(pick, columns, 0.0), axis=1, keepdims=True)[:64]
    row_energy = jnp.broadcast_to(row_energy - occ_ref[wide], (64, 128))
    row_e[...] = row_energy
    for q in range(8):
        row_exp[pl.ds(q * 64, 64), :] = jnp.exp(-kap_ref[q] * row_energy)

    half = ny // 2
    parts = {"all": pl.ds(0, ny), "first": pl.ds(0, half), "second": pl.ds(half, ny - half)}

    def g_copy(p, dx, dz, part, slot, to):
        ref = gath.at[at_batch(dx, dz), p, parts[part], :, core]
        return pltpu.make_async_remote_copy(
            src_ref=ref, dst_ref=ref, send_sem=g_send.at[p, slot], recv_sem=g_recv.at[p, slot],
            device_id=to, device_id_type=MESH,
        )

    sends = {
        0: (right, 0, 0, "all"),
        1: (left, 0, 0, "all"),
        2: (over, 0, 0, "all"),
        3: (right, -1, 0, "first"),
        4: (left, 1, 0, "second"),
        5: (right, 0, 1, "all"),
        6: (left, 0, 1, "all"),
        7: (over, 2, 0, "all"),
    }
    gets = {
        0: (-1, 0, "all"),
        1: (1, 0, "all"),
        2: (0, 1, "all"),
        3: (2, 0, "first"),
        4: (2, 0, "second"),
        5: (-1, 1, "all"),
        6: (1, 1, "all"),
        7: (2, 1, "all"),
    }
    blocks = ((0, 0), (-1, 0), (1, 0), (0, 1), (2, 0), (-1, 1), (1, 1), (2, 1))

    def g_start(p, slot):
        to, dx, dz, part = sends[slot]
        g_copy(p, dx, dz, part, slot, to).start()

    def g_wait(p, slot):
        dx, dz, part = gets[slot]
        g_copy(p, dx, dz, part, slot, right).wait_recv()

    def s_copy(p, block, cc):
        dx, dz = blocks[block]
        ref = gath.at[at_batch(dx, dz), p, :, :, cc]
        return pltpu.make_async_remote_copy(
            src_ref=ref, dst_ref=ref, send_sem=s_send.at[p, block], recv_sem=s_recv.at[p, block],
            device_id=sibling, device_id_type=MESH,
        )

    def s_start(p, block):
        s_copy(p, block, core).start()

    def s_wait(p, block):
        s_copy(p, block, 1 - core).wait_recv()

    def flat(b, p):
        return gath.at[b, p].reshape(naux, 128)

    lane = lax.broadcasted_iota(jnp.int32, (1, 128), 1)
    lane_low = lane < 64
    tn = 256 if naux % 256 == 0 else naux

    def compute(p, first_block, second_block, first, last):
        b0 = at_batch(*blocks[first_block])
        b1 = at_batch(*blocks[second_block])
        r0, r1 = flat(b0, p), flat(b1, p)
        pair = lax.rem(own_pair + p - 1 + pairs, pairs)
        occ_j = jnp.where(lane_low, occ_ref[2 * pair], occ_ref[2 * pair + 1])
        offset = 2 * (p - 1) + jnp.where(lane_low, 0, 1) - core
        keep = jnp.logical_and(offset >= -HALF, offset <= HALF)
        for n, (b, r) in enumerate(((b0, r0), (b1, r1))):
            coulomb = jnp.dot(
                tit[pl.ds(pl.multiple_of(core * 64, 64), 64), :], r[...],
                preferred_element_type=jnp.float32,
            )
            col_e = vir2[pl.ds(b, 1), :] - occ_j
            scaled = -coulomb / (row_e[...] + col_e)
            scaled = jnp.where(keep, scaled, 0.0)
            col_exp = jnp.exp(-kvec[...] * col_e)
            for q in range(8):
                damp = 1.0 - row_exp[pl.ds(q * 64, 64), :] * col_exp[q : q + 1, :]
                amp[pl.ds(q * 64, 64), n * 128 : (n + 1) * 128] = (scaled * (damp * damp)).astype(
                    jnp.bfloat16
                )

        def tile(n, carry):
            at = pl.multiple_of(n * tn, tn)
            rhs = jnp.concatenate([r0[pl.ds(at, tn), :], r1[pl.ds(at, tn), :]], axis=1)
            part = lax.dot_general(
                amp[...], rhs, (((1,), (1,)), ((), ())), preferred_element_type=jnp.float32
            )
            if first:
                acc[:, pl.ds(at, tn)] = part
            elif last:
                out_ref[:, pl.ds(at, tn)] = (acc[:, pl.ds(at, tn)] + part).astype(jnp.bfloat16)
            else:
                acc[:, pl.ds(at, tn)] += part
            return carry

        lax.fori_loop(0, naux // tn, tile, 0)

    def own(p):
        a_wait(p)
        for slot in (0, 1, 2):
            g_start(p, slot)
        s_start(p, 0)

    def near(p):
        g_wait(p, 0)
        g_start(p, 3)
        s_start(p, 1)
        g_wait(p, 1)
        g_start(p, 4)
        s_start(p, 2)
        g_wait(p, 2)
        g_start(p, 5)
        g_start(p, 6)
        s_start(p, 3)

    def opposite(p):
        g_wait(p, 3)
        g_wait(p, 4)
        g_start(p, 7)
        s_start(p, 4)

    def last_of(p):
        for slot, block in ((5, 5), (6, 6), (7, 7)):
            g_wait(p, slot)
            s_start(p, block)

    def shared(p, *which):
        for block in which:
            s_wait(p, block)

    def near_compute(p):
        shared(p, 0, 1, 2, 3)
        if p == 1:
            tit[...] = jnp.transpose(flat(batch, 1)[...])
        compute(p, 0, 3, p == 1, False)
        compute(p, 1, 2, False, False)

    def far_compute(p):
        shared(p, 4, 5, 6, 7)
        compute(p, 5, 6, False, False)
        compute(p, 4, 7, False, p == 2)

    own(1)
    own(0)
    near(1)
    near_compute(1)
    own(2)
    near(0)
    near_compute(0)
    opposite(1)
    near(2)
    near_compute(2)
    opposite(0)
    last_of(1)
    far_compute(1)
    opposite(2)
    last_of(0)
    far_compute(0)
    last_of(2)
    far_compute(2)

    for p in range(3):
        sent = mine.at[pl.ds(0, pairs - 1)]
        pltpu.make_async_copy(sent, sent, a_send.at[p]).wait()
        for slot in range(8):
            to, dx, dz, part = sends[slot]
            g_copy(p, dx, dz, part, slot, to).wait_send()
        for block in range(8):
            s_copy(p, block, core).wait_send()


def on_device(ny, nz, integrals, vir_coeff, occ_energy, vir_energy, kappas):
    aux_local, nocc, basis = integrals.shape
    naux = aux_local * ny * nz * 2
    pairs = ny * nz
    vmem = pl.BlockSpec(memory_space=pltpu.VMEM)
    smem = pl.BlockSpec(memory_space=pltpu.SMEM)
    sub = aux_local // 8
    bf16, f32 = jnp.bfloat16, jnp.float32
    dma = pltpu.SemaphoreType.DMA
    out = pl.pallas_call(
        functools.partial(kernel, ny, nz),
        out_shape=pltpu.VMEM((8 * 64, naux), bf16),
        in_specs=[pl.BlockSpec(memory_space=pl.ANY), vmem, vmem, smem, smem],
        out_specs=vmem,
        scratch_shapes=[
            pltpu.VMEM((aux_local * nocc, basis), bf16),
            pltpu.VMEM((aux_local * nocc, 128), f32),
            pltpu.VMEM((pairs + 2, sub, 8, 128), bf16),
            pltpu.VMEM((2 * NX, 3, ny, nz, 2, sub, 8, 128), bf16),
            pltpu.VMEM((128, naux), bf16),
            pltpu.VMEM((512, 128), f32),
            pltpu.VMEM((8, 128), f32),
            pltpu.VMEM((8, 128), f32),
            pltpu.VMEM((64, 128), f32),
            pltpu.VMEM((512, 256), bf16),
            pltpu.VMEM((512, naux), f32),
            dma((4,)),
            dma((3,)),
            dma((3,)),
            dma((3, 8)),
            dma((3, 8)),
            dma((3, 8)),
            dma((3, 8)),
        ],
        compiler_params=pltpu.CompilerParams(
            collective_id=0, has_side_effects=True, vmem_limit_bytes=60 * 1024 * 1024
        ),
    )(
        integrals.reshape(aux_local * nocc, basis), vir_coeff.T, vir_energy.reshape(1, -1),
        occ_energy, kappas,
    )
    return out.reshape(8, 1, 64, naux)


def solution(mesh):
    wide = mesh.shape["wide"]
    nz = 4 if wide == 64 else 2
    ny = wide // (2 * nz)
    return jax.shard_map(
        functools.partial(on_device, ny, nz),
        mesh=mesh,
        in_specs=(P("wide", None, None), P(None, "batch"), P(), P(), P()),
        out_specs=P(None, "wide", "batch", None),
        check_vma=False,
    )
```

```python
import functools

import jax
import jax.numpy as jnp
from jax import lax
from jax.experimental import pallas as pl
from jax.experimental.pallas import tpu as pltpu
from jax.sharding import PartitionSpec as P

HALF = 2
UNROLL = True
TN = 256
NX = 4
MESH = pl.DeviceIdType.MESH


def kernel(
    ny, nz, ints_in, coef_in, vir_in, occ_in, kap_in, out_ref,
    ints, coef_ref, vir_ref, occ_ref, kap_ref, full, mine, gath, tit, row_exp, vir2, kvec, row_e, amp, acc,
    in_sem, a_send, a_recv, g_send, g_recv, s_send, s_recv,
):
    wide = lax.axis_index("wide")
    batch = lax.axis_index("batch")
    core = lax.rem(wide, 2)
    zh = lax.rem(wide // 2, nz)
    y = wide // (2 * nz)
    x = lax.rem(batch, NX)
    zl = batch // NX
    pairs = ny * nz
    own_pair = wide // 2
    naux = out_ref.shape[1]

    def at_wide(yy, zz, cc):
        return {"wide": (yy * nz + zz) * 2 + cc, "batch": batch}

    def at_batch(dx, dz):
        return lax.rem(zl + dz, 2) * NX + lax.rem(x + dx + NX, NX)

    def dev_batch(dx, dz):
        return {"wide": wide, "batch": at_batch(dx, dz)}

    sibling = at_wide(y, zh, 1 - core)
    left, right, over = dev_batch(-1, 0), dev_batch(1, 0), dev_batch(0, 1)

    barrier = pltpu.get_barrier_semaphore()
    far = sorted(
        ((dy, dz) for dy in range(ny) for dz in range(nz) if (dy, dz) != (0, 0)),
        key=lambda d: -min(d[0], ny - d[0]) - 2 * min(d[1], nz - d[1]),
    )
    owners = [(lax.rem(y + dy, ny), lax.rem(zh + dz, nz)) for dy, dz in far]
    peers = [at_wide(yy, zz, core) for yy, zz in owners]
    peers += [left, right, over, sibling]
    for peer in peers:
        pl.semaphore_signal(barrier, inc=1, device_id=peer, device_id_type=MESH)

    steps = 4
    tall = full.shape[0] // steps

    def fetch(k):
        part = pl.ds(k * tall, tall)
        return pltpu.make_async_copy(ints_in.at[part], ints.at[part], in_sem.at[k])

    small = [
        pltpu.make_async_copy(src, dst, in_sem.at[steps + k])
        for k, (src, dst) in enumerate(
            ((coef_in, coef_ref), (vir_in, vir_ref), (occ_in, occ_ref), (kap_in, kap_ref))
        )
    ]
    small[0].start()
    for k in range(steps):
        fetch(k).start()
    for copy in small[1:]:
        copy.start()
    small[0].wait()
    coef2 = jnp.concatenate([coef_ref[...], coef_ref[...]], axis=0)
    for k in range(steps):
        fetch(k).wait()
        full[pl.ds(k * tall, tall), :] = lax.dot_general(
            ints[pl.ds(k * tall, tall), :], coef2, (((1,), (1,)), ((), ())),
            preferred_element_type=jnp.float32,
        )
    nocc = 2 * pairs
    nrow = full.shape[0] // nocc
    low = lax.broadcasted_iota(jnp.int32, (nrow, 128), 1) < 64
    for m in range(pairs):
        even = full[pl.ds(2 * m, nrow, stride=nocc), :]
        odd = full[pl.ds(2 * m + 1, nrow, stride=nocc), :]
        tile = jnp.where(low, even, odd).reshape(nrow // 8, 8, 128).astype(jnp.bfloat16)
        mine[m + 1] = tile
        if m == 0:
            mine[pairs + 1] = tile
        if m == pairs - 1:
            mine[0] = tile

    pl.semaphore_wait(barrier, len(peers))

    def a_copy(p, yy, zz):
        return pltpu.make_async_remote_copy(
            src_ref=mine.at[yy * nz + zz + p],
            dst_ref=gath.at[batch, p, y, zh, core],
            send_sem=a_send.at[p],
            recv_sem=a_recv.at[p],
            device_id=at_wide(yy, zz, core),
            device_id_type=MESH,
        )

    for p in (1, 0, 2):
        pltpu.make_async_copy(
            mine.at[own_pair + p], gath.at[batch, p, y, zh, core], a_recv.at[p]
        ).start()
        for yy, zz in owners:
            a_copy(p, yy, zz).start()

    def a_wait(p):
        ref = gath.at[batch, p, :, :, core]
        pltpu.make_async_copy(ref, ref, a_recv.at[p]).wait()

    for copy in small[1:]:
        copy.wait()
    for b in range(2 * NX):
        part = vir_ref[:, b * 64 : (b + 1) * 64]
        vir2[pl.ds(b, 1), :] = jnp.concatenate([part, part], axis=1)
    qs = lax.broadcasted_iota(jnp.int32, (8, 128), 0)
    kv = jnp.zeros((8, 128), jnp.float32)
    for q in range(8):
        kv = jnp.where(qs == q, kap_ref[q], kv)
    kvec[...] = kv
    columns = jnp.transpose(vir2[...])
    pick = lax.broadcasted_iota(jnp.int32, (128, 8), 1) == batch
    row_energy = jnp.sum(jnp.where(pick, columns, 0.0), axis=1, keepdims=True)[:64]
    row_energy = jnp.broadcast_to(row_energy - occ_ref[wide], (64, 128))
    row_e[...] = row_energy
    for q in range(8):
        row_exp[pl.ds(q * 64, 64), :] = jnp.exp(-kap_ref[q] * row_energy)

    half = ny // 2
    parts = {"all": pl.ds(0, ny), "first": pl.ds(0, half), "second": pl.ds(half, ny - half)}

    def g_copy(p, dx, dz, part, slot, to):
        ref = gath.at[at_batch(dx, dz), p, parts[part], :, core]
        return pltpu.make_async_remote_copy(
            src_ref=ref, dst_ref=ref, send_sem=g_send.at[p, slot], recv_sem=g_recv.at[p, slot],
            device_id=to, device_id_type=MESH,
        )

    sends = {
        0: (right, 0, 0, "all"),
        1: (left, 0, 0, "all"),
        2: (over, 0, 0, "all"),
        3: (right, -1, 0, "first"),
        4: (left, 1, 0, "second"),
        5: (right, 0, 1, "all"),
        6: (left, 0, 1, "all"),
        7: (over, 2, 0, "all"),
    }
    gets = {
        0: (-1, 0, "all"),
        1: (1, 0, "all"),
        2: (0, 1, "all"),
        3: (2, 0, "first"),
        4: (2, 0, "second"),
        5: (-1, 1, "all"),
        6: (1, 1, "all"),
        7: (2, 1, "all"),
    }
    blocks = ((0, 0), (-1, 0), (1, 0), (0, 1), (2, 0), (-1, 1), (1, 1), (2, 1))

    def g_start(p, slot):
        to, dx, dz, part = sends[slot]
        g_copy(p, dx, dz, part, slot, to).start()

    def g_wait(p, slot):
        dx, dz, part = gets[slot]
        g_copy(p, dx, dz, part, slot, right).wait_recv()

    def s_copy(p, block, cc):
        dx, dz = blocks[block]
        ref = gath.at[at_batch(dx, dz), p, :, :, cc]
        return pltpu.make_async_remote_copy(
            src_ref=ref, dst_ref=ref, send_sem=s_send.at[p, block], recv_sem=s_recv.at[p, block],
            device_id=sibling, device_id_type=MESH,
        )

    def s_start(p, block):
        s_copy(p, block, core).start()

    def s_wait(p, block):
        s_copy(p, block, 1 - core).wait_recv()

    def flat(b, p):
        return gath.at[b, p].reshape(naux, 128)

    lane = lax.broadcasted_iota(jnp.int32, (1, 128), 1)
    lane_low = lane < 64
    tn = TN if naux % TN == 0 else naux

    def compute(p, first_block, second_block, first, last):
        b0 = at_batch(*blocks[first_block])
        b1 = at_batch(*blocks[second_block])
        r0, r1 = flat(b0, p), flat(b1, p)
        pair = lax.rem(own_pair + p - 1 + pairs, pairs)
        occ_j = jnp.where(lane_low, occ_ref[2 * pair], occ_ref[2 * pair + 1])
        offset = 2 * (p - 1) + jnp.where(lane_low, 0, 1) - core
        keep = jnp.logical_and(offset >= -HALF, offset <= HALF)
        col_e = jnp.concatenate([vir2[pl.ds(b, 1), :] - occ_j for b in (b0, b1)], axis=1)
        coulomb = jnp.dot(
            tit[pl.ds(pl.multiple_of(core * 64, 64), 64), :],
            jnp.concatenate([r0[...], r1[...]], axis=1),
            preferred_element_type=jnp.float32,
        )
        rows_e = jnp.concatenate([row_e[...]] * 2, axis=1)
        scaled = -coulomb / (rows_e + col_e)
        scaled = jnp.where(jnp.concatenate([keep] * 2, axis=1), scaled, 0.0)
        col_exp = jnp.exp(-jnp.concatenate([kvec[...]] * 2, axis=1) * col_e)
        for q in range(8):
            grown = row_exp[pl.ds(q * 64, 64), :]
            damp = 1.0 - jnp.concatenate([grown] * 2, axis=1) * col_exp[q : q + 1, :]
            amp[pl.ds(q * 64, 64), :] = (scaled * (damp * damp)).astype(jnp.bfloat16)

        def tile(n, carry):
            at = n * tn if isinstance(n, int) else pl.multiple_of(n * tn, tn)
            rhs = jnp.concatenate([r0[pl.ds(at, tn), :], r1[pl.ds(at, tn), :]], axis=1)
            part = lax.dot_general(
                amp[...], rhs, (((1,), (1,)), ((), ())), preferred_element_type=jnp.float32
            )
            if first:
                acc[:, pl.ds(at, tn)] = part
            elif last:
                out_ref[:, pl.ds(at, tn)] = (acc[:, pl.ds(at, tn)] + part).astype(jnp.bfloat16)
            else:
                acc[:, pl.ds(at, tn)] += part
            return carry

        if UNROLL:
            for n in range(naux // tn):
                tile(n, 0)
        else:
            lax.fori_loop(0, naux // tn, tile, 0)

    def own(p):
        a_wait(p)
        for slot in (0, 1, 2):
            g_start(p, slot)
        s_start(p, 0)

    def near(p):
        g_wait(p, 0)
        g_start(p, 3)
        s_start(p, 1)
        g_wait(p, 1)
        g_start(p, 4)
        s_start(p, 2)

    def across(p):
        g_wait(p, 2)
        g_start(p, 5)
        g_start(p, 6)
        s_start(p, 3)

    def opposite(p):
        g_wait(p, 3)
        g_wait(p, 4)
        g_start(p, 7)
        s_start(p, 4)

    def corners(p):
        for slot, block in ((5, 5), (6, 6)):
            g_wait(p, slot)
            s_start(p, block)

    def far_corner(p):
        g_wait(p, 7)
        s_start(p, 7)

    def step(p, first_block, second_block, first=False, last=False):
        for block in (first_block, second_block):
            s_wait(p, block)
        compute(p, first_block, second_block, first, last)

    def compute_own(p):
        if p != 1:
            s_wait(p, 0)
        s_wait(p, 3)
        compute(p, 0, 3, False, False)

    own(1)
    own(0)
    near(1)
    own(2)
    s_wait(1, 0)
    tit[...] = jnp.transpose(flat(batch, 1)[...])
    step(1, 1, 2, first=True)
    near(0)
    step(0, 1, 2)
    near(2)
    across(1)
    compute_own(1)
    opposite(1)
    step(2, 1, 2)
    across(0)
    compute_own(0)
    corners(1)
    opposite(0)
    across(2)
    step(1, 5, 6)
    compute_own(2)
    far_corner(1)
    step(1, 4, 7)
    corners(0)
    opposite(2)
    step(0, 5, 6)
    far_corner(0)
    step(0, 4, 7)
    corners(2)
    step(2, 5, 6)
    far_corner(2)
    step(2, 4, 7, last=True)

    for p in range(3):
        sent = mine.at[pl.ds(0, pairs - 1)]
        pltpu.make_async_copy(sent, sent, a_send.at[p]).wait()
        for slot in range(8):
            to, dx, dz, part = sends[slot]
            g_copy(p, dx, dz, part, slot, to).wait_send()
        for block in range(8):
            s_copy(p, block, core).wait_send()


def on_device(ny, nz, integrals, vir_coeff, occ_energy, vir_energy, kappas):
    aux_local, nocc, basis = integrals.shape
    naux = aux_local * ny * nz * 2
    pairs = ny * nz
    vmem = pl.BlockSpec(memory_space=pltpu.VMEM)
    sub = aux_local // 8
    bf16, f32 = jnp.bfloat16, jnp.float32
    dma = pltpu.SemaphoreType.DMA
    out = pl.pallas_call(
        functools.partial(kernel, ny, nz),
        out_shape=pltpu.VMEM((8 * 64, naux), bf16),
        in_specs=[pl.BlockSpec(memory_space=pl.ANY)] * 5,
        out_specs=vmem,
        scratch_shapes=[
            pltpu.VMEM((aux_local * nocc, basis), bf16),
            pltpu.VMEM((64, basis), bf16),
            pltpu.VMEM((1, 2 * NX * 64), f32),
            pltpu.SMEM((nocc,), f32),
            pltpu.SMEM((8,), f32),
            pltpu.VMEM((aux_local * nocc, 128), f32),
            pltpu.VMEM((pairs + 2, sub, 8, 128), bf16),
            pltpu.VMEM((2 * NX, 3, ny, nz, 2, sub, 8, 128), bf16),
            pltpu.VMEM((128, naux), bf16),
            pltpu.VMEM((512, 128), f32),
            pltpu.VMEM((8, 128), f32),
            pltpu.VMEM((8, 128), f32),
            pltpu.VMEM((64, 128), f32),
            pltpu.VMEM((512, 256), bf16),
            pltpu.VMEM((512, naux), f32),
            dma((8,)),
            dma((3,)),
            dma((3,)),
            dma((3, 8)),
            dma((3, 8)),
            dma((3, 8)),
            dma((3, 8)),
        ],
        compiler_params=pltpu.CompilerParams(
            collective_id=0, has_side_effects=True, vmem_limit_bytes=60 * 1024 * 1024
        ),
    )(
        integrals.reshape(aux_local * nocc, basis), vir_coeff.T, vir_energy.reshape(1, -1),
        occ_energy, kappas,
    )
    return out.reshape(8, 1, 64, naux)


def solution(mesh):
    wide = mesh.shape["wide"]
    nz = 4 if wide == 64 else 2
    ny = wide // (2 * nz)
    return jax.shard_map(
        functools.partial(on_device, ny, nz),
        mesh=mesh,
        in_specs=(P("wide", None, None), P(None, "batch"), P(), P(), P()),
        out_specs=P(None, "wide", "batch", None),
        check_vma=False,
    )
```

```python
import functools

import jax
import jax.numpy as jnp
from jax import lax
from jax.experimental import pallas as pl
from jax.experimental.pallas import tpu as pltpu
from jax.sharding import PartitionSpec as P

HALF = 2
TN = 256
NX = 4
MESH = pl.DeviceIdType.MESH


def kernel(
    ny, nz, ints_in, coef_in, vir_in, occ_in, kap_in, out_ref,
    ints, coef_ref, vir_ref, occ_ref, kap_ref, full, mine, gath, tit, row_exp, vir2, kvec, row_e, amp, acc,
    in_sem, a_send, a_recv, e_send, g_send, g_recv, s_send, s_recv,
):
    wide = lax.axis_index("wide")
    batch = lax.axis_index("batch")
    core = lax.rem(wide, 2)
    zh = lax.rem(wide // 2, nz)
    y = wide // (2 * nz)
    x = lax.rem(batch, NX)
    zl = batch // NX
    pairs = ny * nz
    own_pair = wide // 2
    naux = out_ref.shape[1]

    def at_wide(yy, zz, cc):
        return {"wide": (yy * nz + zz) * 2 + cc, "batch": batch}

    def at_batch(dx, dz):
        return lax.rem(zl + dz, 2) * NX + lax.rem(x + dx + NX, NX)

    def dev_batch(dx, dz):
        return {"wide": wide, "batch": at_batch(dx, dz)}

    sibling = at_wide(y, zh, 1 - core)
    left, right, over = dev_batch(-1, 0), dev_batch(1, 0), dev_batch(0, 1)
    beyond = {
        "wide": 2 * lax.rem(own_pair + 2 * zl - 1 + pairs, pairs) + core,
        "batch": at_batch(0, 1),
    }
    centre, shared, other = 1, 2 * zl, 2 - 2 * zl
    order = (centre, shared, other)

    barrier = pltpu.get_barrier_semaphore()
    far = sorted(
        ((dy, dz) for dy in range(ny) for dz in range(nz) if (dy, dz) != (0, 0)),
        key=lambda d: -min(d[0], ny - d[0]) - 2 * min(d[1], nz - d[1]),
    )
    owners = [(lax.rem(y + dy, ny), lax.rem(zh + dz, nz)) for dy, dz in far]
    peers = [at_wide(yy, zz, core) for yy, zz in owners]
    peers += [left, right, over, sibling, beyond]
    for peer in peers:
        pl.semaphore_signal(barrier, inc=1, device_id=peer, device_id_type=MESH)

    steps = 4
    tall = full.shape[0] // steps

    def fetch(k):
        part = pl.ds(k * tall, tall)
        return pltpu.make_async_copy(ints_in.at[part], ints.at[part], in_sem.at[k])

    small = [
        pltpu.make_async_copy(src, dst, in_sem.at[steps + k])
        for k, (src, dst) in enumerate(
            ((coef_in, coef_ref), (vir_in, vir_ref), (occ_in, occ_ref), (kap_in, kap_ref))
        )
    ]
    small[0].start()
    for k in range(steps):
        fetch(k).start()
    for copy in small[1:]:
        copy.start()
    small[0].wait()
    coef2 = jnp.concatenate([coef_ref[...], coef_ref[...]], axis=0)
    for k in range(steps):
        fetch(k).wait()
        full[pl.ds(k * tall, tall), :] = lax.dot_general(
            ints[pl.ds(k * tall, tall), :], coef2, (((1,), (1,)), ((), ())),
            preferred_element_type=jnp.float32,
        )
    nocc = 2 * pairs
    nrow = full.shape[0] // nocc
    low = lax.broadcasted_iota(jnp.int32, (nrow, 128), 1) < 64
    for m in range(pairs):
        even = full[pl.ds(2 * m, nrow, stride=nocc), :]
        odd = full[pl.ds(2 * m + 1, nrow, stride=nocc), :]
        tile = jnp.where(low, even, odd).reshape(nrow // 8, 8, 128).astype(jnp.bfloat16)
        mine[m + 1] = tile
        if m == 0:
            mine[pairs + 1] = tile
        if m == pairs - 1:
            mine[0] = tile

    pl.semaphore_wait(barrier, len(peers))

    def a_copy(p, yy, zz):
        return pltpu.make_async_remote_copy(
            src_ref=mine.at[yy * nz + zz + p],
            dst_ref=gath.at[batch, p, y, zh, core],
            send_sem=a_send.at[p],
            recv_sem=a_recv.at[p],
            device_id=at_wide(yy, zz, core),
            device_id_type=MESH,
        )

    for p in order:
        pltpu.make_async_copy(
            mine.at[own_pair + p], gath.at[batch, p, y, zh, core], a_recv.at[p]
        ).start()
        for yy, zz in owners:
            a_copy(p, yy, zz).start()

    def a_wait(p):
        ref = gath.at[batch, p, :, :, core]
        pltpu.make_async_copy(ref, ref, a_recv.at[p]).wait()

    for copy in small[1:]:
        copy.wait()
    for b in range(2 * NX):
        part = vir_ref[:, b * 64 : (b + 1) * 64]
        vir2[pl.ds(b, 1), :] = jnp.concatenate([part, part], axis=1)
    qs = lax.broadcasted_iota(jnp.int32, (8, 128), 0)
    kv = jnp.zeros((8, 128), jnp.float32)
    for q in range(8):
        kv = jnp.where(qs == q, kap_ref[q], kv)
    kvec[...] = kv
    columns = jnp.transpose(vir2[...])
    pick = lax.broadcasted_iota(jnp.int32, (128, 8), 1) == batch
    row_energy = jnp.sum(jnp.where(pick, columns, 0.0), axis=1, keepdims=True)[:64]
    row_energy = jnp.broadcast_to(row_energy - occ_ref[wide], (64, 128))
    row_e[...] = row_energy
    for q in range(8):
        row_exp[pl.ds(q * 64, 64), :] = jnp.exp(-kap_ref[q] * row_energy)

    half = ny // 2
    parts = {"all": pl.ds(0, ny), "first": pl.ds(0, half), "second": pl.ds(half, ny - half)}

    def g_copy(p, dx, dz, part, slot, to):
        ref = gath.at[at_batch(dx, dz), p, parts[part], :, core]
        return pltpu.make_async_remote_copy(
            src_ref=ref, dst_ref=ref, send_sem=g_send.at[p, slot], recv_sem=g_recv.at[p, slot],
            device_id=to, device_id_type=MESH,
        )

    def e_copy(k):
        dx, p, to_p, slot = (
            (-1, centre, other, 5),
            (1, centre, other, 6),
            (2, centre, other, 7),
            (2, shared, centre, 7),
        )[k]
        b = at_batch(dx, 0)
        return pltpu.make_async_remote_copy(
            src_ref=gath.at[b, p, :, :, core], dst_ref=gath.at[b, to_p, :, :, core],
            send_sem=e_send.at[k], recv_sem=g_recv.at[to_p, slot],
            device_id=beyond, device_id_type=MESH,
        )

    sends = {
        0: (right, 0, 0, "all"),
        1: (left, 0, 0, "all"),
        2: (over, 0, 0, "all"),
        3: (right, -1, 0, "first"),
        4: (left, 1, 0, "second"),
        5: (right, 0, 1, "all"),
        6: (left, 0, 1, "all"),
        7: (over, 2, 0, "all"),
    }
    gets = {
        0: (-1, 0, "all"),
        1: (1, 0, "all"),
        2: (0, 1, "all"),
        3: (2, 0, "first"),
        4: (2, 0, "second"),
        5: (-1, 1, "all"),
        6: (1, 1, "all"),
        7: (2, 1, "all"),
    }
    blocks = ((0, 0), (-1, 0), (1, 0), (0, 1), (2, 0), (-1, 1), (1, 1), (2, 1))

    def g_start(p, slot):
        to, dx, dz, part = sends[slot]
        g_copy(p, dx, dz, part, slot, to).start()

    def g_wait(p, slot):
        dx, dz, part = gets[slot]
        g_copy(p, dx, dz, part, slot, right).wait_recv()

    def s_copy(p, block, cc):
        dx, dz = blocks[block]
        ref = gath.at[at_batch(dx, dz), p, :, :, cc]
        return pltpu.make_async_remote_copy(
            src_ref=ref, dst_ref=ref, send_sem=s_send.at[p, block], recv_sem=s_recv.at[p, block],
            device_id=sibling, device_id_type=MESH,
        )

    def s_start(p, block):
        s_copy(p, block, core).start()

    def s_wait(p, block):
        s_copy(p, block, 1 - core).wait_recv()

    def flat(b, p):
        return gath.at[b, p].reshape(naux, 128)

    lane = lax.broadcasted_iota(jnp.int32, (1, 128), 1)
    lane_low = lane < 64
    tn = TN if naux % TN == 0 else naux

    def compute(p, first_block, second_block, first, last):
        b0 = at_batch(*blocks[first_block])
        b1 = at_batch(*blocks[second_block])
        r0, r1 = flat(b0, p), flat(b1, p)
        pair = lax.rem(own_pair + p - 1 + pairs, pairs)
        occ_j = jnp.where(lane_low, occ_ref[2 * pair], occ_ref[2 * pair + 1])
        offset = 2 * (p - 1) + jnp.where(lane_low, 0, 1) - core
        keep = jnp.logical_and(offset >= -HALF, offset <= HALF)
        col_e = jnp.concatenate([vir2[pl.ds(b, 1), :] - occ_j for b in (b0, b1)], axis=1)
        coulomb = jnp.dot(
            tit[pl.ds(pl.multiple_of(core * 64, 64), 64), :],
            jnp.concatenate([r0[...], r1[...]], axis=1),
            preferred_element_type=jnp.float32,
        )
        rows_e = jnp.concatenate([row_e[...]] * 2, axis=1)
        scaled = -coulomb / (rows_e + col_e)
        scaled = jnp.where(jnp.concatenate([keep] * 2, axis=1), scaled, 0.0)
        col_exp = jnp.exp(-jnp.concatenate([kvec[...]] * 2, axis=1) * col_e)
        for q in range(8):
            grown = row_exp[pl.ds(q * 64, 64), :]
            damp = 1.0 - jnp.concatenate([grown] * 2, axis=1) * col_exp[q : q + 1, :]
            amp[pl.ds(q * 64, 64), :] = (scaled * (damp * damp)).astype(jnp.bfloat16)

        def tile(n):
            at = n * tn
            rhs = jnp.concatenate([r0[pl.ds(at, tn), :], r1[pl.ds(at, tn), :]], axis=1)
            part = lax.dot_general(
                amp[...], rhs, (((1,), (1,)), ((), ())), preferred_element_type=jnp.float32
            )
            if first:
                acc[:, pl.ds(at, tn)] = part
            elif last:
                out_ref[:, pl.ds(at, tn)] = (acc[:, pl.ds(at, tn)] + part).astype(jnp.bfloat16)
            else:
                acc[:, pl.ds(at, tn)] += part

        for n in range(naux // tn):
            tile(n)

    def own(p):
        a_wait(p)
        for slot in (0, 1, 2):
            g_start(p, slot)
        s_start(p, 0)

    def near(p):
        g_wait(p, 0)
        g_start(p, 3)
        s_start(p, 1)
        g_wait(p, 1)
        g_start(p, 4)
        s_start(p, 2)
        if p is centre:
            e_copy(0).start()
            e_copy(1).start()

    def across(p):
        g_wait(p, 2)
        if p is not shared:
            g_start(p, 5)
            g_start(p, 6)
        s_start(p, 3)

    def opposite(p):
        g_wait(p, 3)
        g_wait(p, 4)
        if p is centre:
            e_copy(2).start()
        elif p is shared:
            e_copy(3).start()
            g_start(p, 7)
        s_start(p, 4)

    def corners(p):
        for slot, block in ((5, 5), (6, 6)):
            g_wait(p, slot)
            s_start(p, block)

    def far_corner(p):
        g_wait(p, 7)
        s_start(p, 7)

    def step(p, first_block, second_block, first=False, last=False):
        for block in (first_block, second_block):
            if (p is centre, block) != (True, 0):
                s_wait(p, block)
        compute(p, first_block, second_block, first, last)

    own(centre)
    own(shared)
    near(centre)
    own(other)
    s_wait(centre, 0)
    tit[...] = jnp.transpose(flat(batch, centre)[...])
    step(centre, 1, 2, first=True)
    near(shared)
    step(shared, 1, 2)
    near(other)
    across(centre)
    opposite(centre)
    step(centre, 0, 3)
    step(other, 1, 2)
    opposite(shared)
    across(other)
    step(other, 0, 3)
    corners(shared)
    step(shared, 5, 6)
    opposite(other)
    across(shared)
    corners(centre)
    step(shared, 0, 3)
    step(centre, 5, 6)
    far_corner(shared)
    step(shared, 4, 7)
    far_corner(centre)
    far_corner(other)
    step(centre, 4, 7)
    corners(other)
    step(other, 4, 7)
    step(other, 5, 6, last=True)

    for p in range(3):
        sent = mine.at[pl.ds(0, pairs - 1)]
        pltpu.make_async_copy(sent, sent, a_send.at[p]).wait()
        for block in range(8):
            s_copy(p, block, core).wait_send()
    for p, slots in ((centre, range(7)), (shared, (0, 1, 2, 3, 4, 7)), (other, range(7))):
        for slot in slots:
            to, dx, dz, part = sends[slot]
            g_copy(p, dx, dz, part, slot, to).wait_send()
    for k in range(4):
        e_copy(k).wait_send()


def on_device(ny, nz, integrals, vir_coeff, occ_energy, vir_energy, kappas):
    aux_local, nocc, basis = integrals.shape
    naux = aux_local * ny * nz * 2
    pairs = ny * nz
    vmem = pl.BlockSpec(memory_space=pltpu.VMEM)
    sub = aux_local // 8
    bf16, f32 = jnp.bfloat16, jnp.float32
    dma = pltpu.SemaphoreType.DMA
    out = pl.pallas_call(
        functools.partial(kernel, ny, nz),
        out_shape=pltpu.VMEM((8 * 64, naux), bf16),
        in_specs=[pl.BlockSpec(memory_space=pl.ANY)] * 5,
        out_specs=vmem,
        scratch_shapes=[
            pltpu.VMEM((aux_local * nocc, basis), bf16),
            pltpu.VMEM((64, basis), bf16),
            pltpu.VMEM((1, 2 * NX * 64), f32),
            pltpu.SMEM((nocc,), f32),
            pltpu.SMEM((8,), f32),
            pltpu.VMEM((aux_local * nocc, 128), f32),
            pltpu.VMEM((pairs + 2, sub, 8, 128), bf16),
            pltpu.VMEM((2 * NX, 3, ny, nz, 2, sub, 8, 128), bf16),
            pltpu.VMEM((128, naux), bf16),
            pltpu.VMEM((512, 128), f32),
            pltpu.VMEM((8, 128), f32),
            pltpu.VMEM((8, 128), f32),
            pltpu.VMEM((64, 128), f32),
            pltpu.VMEM((512, 256), bf16),
            pltpu.VMEM((512, naux), f32),
            dma((8,)),
            dma((3,)),
            dma((3,)),
            dma((4,)),
            dma((3, 8)),
            dma((3, 8)),
            dma((3, 8)),
            dma((3, 8)),
        ],
        compiler_params=pltpu.CompilerParams(
            collective_id=0, has_side_effects=True, vmem_limit_bytes=60 * 1024 * 1024
        ),
    )(
        integrals.reshape(aux_local * nocc, basis), vir_coeff.T, vir_energy.reshape(1, -1),
        occ_energy, kappas,
    )
    return out.reshape(8, 1, 64, naux)


def solution(mesh):
    wide = mesh.shape["wide"]
    nz = 4 if wide == 64 else 2
    ny = wide // (2 * nz)
    return jax.shard_map(
        functools.partial(on_device, ny, nz),
        mesh=mesh,
        in_specs=(P("wide", None, None), P(None, "batch"), P(), P(), P()),
        out_specs=P(None, "wide", "batch", None),
        check_vma=False,
    )
```

```python
import functools

import jax
import jax.numpy as jnp
from jax import lax
from jax.experimental import pallas as pl
from jax.experimental.pallas import tpu as pltpu
from jax.sharding import PartitionSpec as P

HALF = 2
TN = 256
NX = 4
MESH = pl.DeviceIdType.MESH


def kernel(
    ny, nz, ints_in, coef_in, vir_in, occ_in, kap_in, out_ref,
    ints, coef_ref, vir_ref, occ_ref, kap_ref, full, mine, gath, tit, row_exp, vir2, kvec, row_e, amp, acc,
    in_sem, a_send, a_recv, c_recv, e_send, g_send, g_recv, s_send, s_recv,
):
    wide = lax.axis_index("wide")
    batch = lax.axis_index("batch")
    core = lax.rem(wide, 2)
    zh = lax.rem(wide // 2, nz)
    y = wide // (2 * nz)
    x = lax.rem(batch, NX)
    zl = batch // NX
    pairs = ny * nz
    own_pair = wide // 2
    naux = out_ref.shape[1]

    def at_wide(yy, zz, cc):
        return {"wide": (yy * nz + zz) * 2 + cc, "batch": batch}

    def at_batch(dx, dz):
        return lax.rem(zl + dz, 2) * NX + lax.rem(x + dx + NX, NX)

    def dev_batch(dx, dz):
        return {"wide": wide, "batch": at_batch(dx, dz)}

    sibling = at_wide(y, zh, 1 - core)
    left, right, over = dev_batch(-1, 0), dev_batch(1, 0), dev_batch(0, 1)
    beyond = {
        "wide": 2 * lax.rem(own_pair + 2 * zl - 1 + pairs, pairs) + core,
        "batch": at_batch(0, 1),
    }
    centre, shared, other = 1, 2 * zl, 2 - 2 * zl
    order = (centre, shared, other)

    barrier = pltpu.get_barrier_semaphore()
    far = sorted(
        ((dy, dz) for dy in range(ny) for dz in range(nz) if (dy, dz) != (0, 0)),
        key=lambda d: -min(d[0], ny - d[0]) - 2 * min(d[1], nz - d[1]),
    )
    owners = [(lax.rem(y + dy, ny), lax.rem(zh + dz, nz)) for dy, dz in far]
    peers = [at_wide(yy, zz, core) for yy, zz in owners]
    peers += [left, right, over, sibling, beyond]
    for peer in peers:
        pl.semaphore_signal(barrier, inc=1, device_id=peer, device_id_type=MESH)

    steps = 4
    tall = full.shape[0] // steps

    def fetch(k):
        part = pl.ds(k * tall, tall)
        return pltpu.make_async_copy(ints_in.at[part], ints.at[part], in_sem.at[k])

    small = [
        pltpu.make_async_copy(src, dst, in_sem.at[steps + k])
        for k, (src, dst) in enumerate(
            ((coef_in, coef_ref), (vir_in, vir_ref), (occ_in, occ_ref), (kap_in, kap_ref))
        )
    ]
    small[0].start()
    for k in range(steps):
        fetch(k).start()
    for copy in small[1:]:
        copy.start()
    small[0].wait()
    coef2 = jnp.concatenate([coef_ref[...], coef_ref[...]], axis=0)
    for k in range(steps):
        fetch(k).wait()
        full[pl.ds(k * tall, tall), :] = lax.dot_general(
            ints[pl.ds(k * tall, tall), :], coef2, (((1,), (1,)), ((), ())),
            preferred_element_type=jnp.float32,
        )
    nocc = 2 * pairs
    nrow = full.shape[0] // nocc
    low = lax.broadcasted_iota(jnp.int32, (nrow, 128), 1) < 64
    for m in range(pairs):
        even = full[pl.ds(2 * m, nrow, stride=nocc), :]
        odd = full[pl.ds(2 * m + 1, nrow, stride=nocc), :]
        tile = jnp.where(low, even, odd).reshape(nrow // 8, 8, 128).astype(jnp.bfloat16)
        mine[m + 1] = tile
        if m == 0:
            mine[pairs + 1] = tile
        if m == pairs - 1:
            mine[0] = tile

    pl.semaphore_wait(barrier, len(peers))

    def a_copy(p, yy, zz):
        return pltpu.make_async_remote_copy(
            src_ref=mine.at[yy * nz + zz + p],
            dst_ref=gath.at[batch, p, y, zh, core],
            send_sem=a_send.at[p],
            recv_sem=c_recv.at[y] if p is centre else a_recv.at[p],
            device_id=at_wide(yy, zz, core),
            device_id_type=MESH,
        )

    for p in order:
        pltpu.make_async_copy(
            mine.at[own_pair + p], gath.at[batch, p, y, zh, core],
            c_recv.at[y] if p is centre else a_recv.at[p],
        ).start()
        for yy, zz in owners:
            a_copy(p, yy, zz).start()

    def a_wait(p):
        ref = gath.at[batch, p, :, :, core]
        pltpu.make_async_copy(ref, ref, a_recv.at[p]).wait()

    for copy in small[1:]:
        copy.wait()
    for b in range(2 * NX):
        part = vir_ref[:, b * 64 : (b + 1) * 64]
        vir2[pl.ds(b, 1), :] = jnp.concatenate([part, part], axis=1)
    qs = lax.broadcasted_iota(jnp.int32, (8, 128), 0)
    kv = jnp.zeros((8, 128), jnp.float32)
    for q in range(8):
        kv = jnp.where(qs == q, kap_ref[q], kv)
    kvec[...] = kv
    columns = jnp.transpose(vir2[...])
    pick = lax.broadcasted_iota(jnp.int32, (128, 8), 1) == batch
    row_energy = jnp.sum(jnp.where(pick, columns, 0.0), axis=1, keepdims=True)[:64]
    row_energy = jnp.broadcast_to(row_energy - occ_ref[wide], (64, 128))
    row_e[...] = row_energy
    for q in range(8):
        row_exp[pl.ds(q * 64, 64), :] = jnp.exp(-kap_ref[q] * row_energy)

    half = ny // 2
    parts = {"all": pl.ds(0, ny), "first": pl.ds(0, half), "second": pl.ds(half, ny - half)}

    def g_copy(p, dx, dz, part, slot, to):
        ref = gath.at[at_batch(dx, dz), p, parts[part], :, core]
        return pltpu.make_async_remote_copy(
            src_ref=ref, dst_ref=ref, send_sem=g_send.at[p, slot], recv_sem=g_recv.at[p, slot],
            device_id=to, device_id_type=MESH,
        )

    def e_copy(k):
        dx, p, to_p, slot = (
            (-1, centre, other, 5),
            (1, centre, other, 6),
            (2, centre, other, 7),
            (2, shared, centre, 7),
        )[k]
        b = at_batch(dx, 0)
        return pltpu.make_async_remote_copy(
            src_ref=gath.at[b, p, :, :, core], dst_ref=gath.at[b, to_p, :, :, core],
            send_sem=e_send.at[k], recv_sem=g_recv.at[to_p, slot],
            device_id=beyond, device_id_type=MESH,
        )

    sends = {
        0: (right, 0, 0, "all"),
        1: (left, 0, 0, "all"),
        2: (over, 0, 0, "all"),
        3: (right, -1, 0, "first"),
        4: (left, 1, 0, "second"),
        5: (right, 0, 1, "all"),
        6: (left, 0, 1, "all"),
        7: (over, 2, 0, "all"),
    }
    gets = {
        0: (-1, 0, "all"),
        1: (1, 0, "all"),
        2: (0, 1, "all"),
        3: (2, 0, "first"),
        4: (2, 0, "second"),
        5: (-1, 1, "all"),
        6: (1, 1, "all"),
        7: (2, 1, "all"),
    }
    blocks = ((0, 0), (-1, 0), (1, 0), (0, 1), (2, 0), (-1, 1), (1, 1), (2, 1))

    def g_start(p, slot):
        to, dx, dz, part = sends[slot]
        g_copy(p, dx, dz, part, slot, to).start()

    def g_wait(p, slot):
        dx, dz, part = gets[slot]
        g_copy(p, dx, dz, part, slot, right).wait_recv()

    def s_copy(p, block, cc):
        dx, dz = blocks[block]
        ref = gath.at[at_batch(dx, dz), p, :, :, cc]
        return pltpu.make_async_remote_copy(
            src_ref=ref, dst_ref=ref, send_sem=s_send.at[p, block], recv_sem=s_recv.at[p, block],
            device_id=sibling, device_id_type=MESH,
        )

    def s_start(p, block):
        s_copy(p, block, core).start()

    def s_wait(p, block):
        s_copy(p, block, 1 - core).wait_recv()

    def flat(b, p):
        return gath.at[b, p].reshape(naux, 128)

    lane = lax.broadcasted_iota(jnp.int32, (1, 128), 1)
    lane_low = lane < 64
    tn = TN if naux % TN == 0 else naux

    def compute(p, first_block, second_block, first, last):
        b0 = at_batch(*blocks[first_block])
        b1 = at_batch(*blocks[second_block])
        r0, r1 = flat(b0, p), flat(b1, p)
        pair = lax.rem(own_pair + p - 1 + pairs, pairs)
        occ_j = jnp.where(lane_low, occ_ref[2 * pair], occ_ref[2 * pair + 1])
        offset = 2 * (p - 1) + jnp.where(lane_low, 0, 1) - core
        keep = jnp.logical_and(offset >= -HALF, offset <= HALF)
        col_e = jnp.concatenate([vir2[pl.ds(b, 1), :] - occ_j for b in (b0, b1)], axis=1)
        coulomb = jnp.dot(
            tit[pl.ds(pl.multiple_of(core * 64, 64), 64), :],
            jnp.concatenate([r0[...], r1[...]], axis=1),
            preferred_element_type=jnp.float32,
        )
        rows_e = jnp.concatenate([row_e[...]] * 2, axis=1)
        scaled = -coulomb / (rows_e + col_e)
        scaled = jnp.where(jnp.concatenate([keep] * 2, axis=1), scaled, 0.0)
        col_exp = jnp.exp(-jnp.concatenate([kvec[...]] * 2, axis=1) * col_e)
        for q in range(8):
            grown = row_exp[pl.ds(q * 64, 64), :]
            damp = 1.0 - jnp.concatenate([grown] * 2, axis=1) * col_exp[q : q + 1, :]
            amp[pl.ds(q * 64, 64), :] = (scaled * (damp * damp)).astype(jnp.bfloat16)

        def tile(n):
            at = n * tn
            rhs = jnp.concatenate([r0[pl.ds(at, tn), :], r1[pl.ds(at, tn), :]], axis=1)
            part = lax.dot_general(
                amp[...], rhs, (((1,), (1,)), ((), ())), preferred_element_type=jnp.float32
            )
            if first:
                acc[:, pl.ds(at, tn)] = part
            elif last:
                out_ref[:, pl.ds(at, tn)] = (acc[:, pl.ds(at, tn)] + part).astype(jnp.bfloat16)
            else:
                acc[:, pl.ds(at, tn)] += part

        for n in range(naux // tn):
            tile(n)

    def own(p):
        if p is centre:
            for d in sorted(range(ny), key=lambda d: min(d, ny - d)):
                row = lax.rem(y + d, ny)
                ref = gath.at[batch, p, row, :, core]
                pltpu.make_async_copy(ref, ref, c_recv.at[row]).wait()
                for slot in (0, 1):
                    pltpu.make_async_remote_copy(
                        src_ref=ref, dst_ref=ref,
                        send_sem=g_send.at[p, slot], recv_sem=g_recv.at[p, slot],
                        device_id=sends[slot][0], device_id_type=MESH,
                    ).start()
        else:
            a_wait(p)
            g_start(p, 0)
            g_start(p, 1)
        g_start(p, 2)
        s_start(p, 0)

    def near(p):
        g_wait(p, 0)
        if p is not other:
            g_start(p, 3)
        s_start(p, 1)
        g_wait(p, 1)
        if p is not other:
            g_start(p, 4)
        s_start(p, 2)
        if p is centre:
            e_copy(0).start()
            e_copy(1).start()

    def across(p):
        g_wait(p, 2)
        if p is not shared:
            g_start(p, 5)
            g_start(p, 6)
        if p is other:
            g_start(p, 3)
            g_start(p, 4)
        s_start(p, 3)

    def opposite(p):
        g_wait(p, 3)
        g_wait(p, 4)
        if p is centre:
            e_copy(2).start()
        elif p is shared:
            e_copy(3).start()
            g_start(p, 7)
        s_start(p, 4)

    def corners(p):
        for slot, block in ((5, 5), (6, 6)):
            g_wait(p, slot)
            s_start(p, block)

    def far_corner(p):
        g_wait(p, 7)
        s_start(p, 7)

    def step(p, first_block, second_block, first=False, last=False):
        for block in (first_block, second_block):
            if (p is centre, block) != (True, 0):
                s_wait(p, block)
        compute(p, first_block, second_block, first, last)

    own(centre)
    own(shared)
    near(centre)
    own(other)
    s_wait(centre, 0)
    tit[...] = jnp.transpose(flat(batch, centre)[...])
    near(shared)
    step(centre, 1, 2, first=True)
    near(other)
    across(centre)
    step(shared, 1, 2)
    opposite(centre)
    step(centre, 0, 3)
    across(other)
    opposite(shared)
    corners(shared)
    step(other, 1, 2)
    step(other, 0, 3)
    step(shared, 5, 6)
    across(shared)
    far_corner(shared)
    corners(centre)
    step(shared, 0, 3)
    step(shared, 4, 7)
    corners(other)
    step(centre, 5, 6)
    far_corner(centre)
    far_corner(other)
    opposite(other)
    step(other, 5, 6)
    step(centre, 4, 7)
    step(other, 4, 7, last=True)

    for p in range(3):
        sent = mine.at[pl.ds(0, pairs - 1)]
        pltpu.make_async_copy(sent, sent, a_send.at[p]).wait()
        for block in range(8):
            s_copy(p, block, core).wait_send()
    for p, slots in ((centre, range(7)), (shared, (0, 1, 2, 3, 4, 7)), (other, range(7))):
        for slot in slots:
            to, dx, dz, part = sends[slot]
            g_copy(p, dx, dz, part, slot, to).wait_send()
    for k in range(4):
        e_copy(k).wait_send()


def on_device(ny, nz, integrals, vir_coeff, occ_energy, vir_energy, kappas):
    aux_local, nocc, basis = integrals.shape
    naux = aux_local * ny * nz * 2
    pairs = ny * nz
    vmem = pl.BlockSpec(memory_space=pltpu.VMEM)
    sub = aux_local // 8
    bf16, f32 = jnp.bfloat16, jnp.float32
    dma = pltpu.SemaphoreType.DMA
    out = pl.pallas_call(
        functools.partial(kernel, ny, nz),
        out_shape=pltpu.VMEM((8 * 64, naux), bf16),
        in_specs=[pl.BlockSpec(memory_space=pl.ANY)] * 5,
        out_specs=vmem,
        scratch_shapes=[
            pltpu.VMEM((aux_local * nocc, basis), bf16),
            pltpu.VMEM((64, basis), bf16),
            pltpu.VMEM((1, 2 * NX * 64), f32),
            pltpu.SMEM((nocc,), f32),
            pltpu.SMEM((8,), f32),
            pltpu.VMEM((aux_local * nocc, 128), f32),
            pltpu.VMEM((pairs + 2, sub, 8, 128), bf16),
            pltpu.VMEM((2 * NX, 3, ny, nz, 2, sub, 8, 128), bf16),
            pltpu.VMEM((128, naux), bf16),
            pltpu.VMEM((512, 128), f32),
            pltpu.VMEM((8, 128), f32),
            pltpu.VMEM((8, 128), f32),
            pltpu.VMEM((64, 128), f32),
            pltpu.VMEM((512, 256), bf16),
            pltpu.VMEM((512, naux), f32),
            dma((8,)),
            dma((3,)),
            dma((3,)),
            dma((ny,)),
            dma((4,)),
            dma((3, 8)),
            dma((3, 8)),
            dma((3, 8)),
            dma((3, 8)),
        ],
        compiler_params=pltpu.CompilerParams(
            collective_id=0, has_side_effects=True, vmem_limit_bytes=60 * 1024 * 1024
        ),
    )(
        integrals.reshape(aux_local * nocc, basis), vir_coeff.T, vir_energy.reshape(1, -1),
        occ_energy, kappas,
    )
    return out.reshape(8, 1, 64, naux)


def solution(mesh):
    wide = mesh.shape["wide"]
    nz = 4 if wide == 64 else 2
    ny = wide // (2 * nz)
    return jax.shard_map(
        functools.partial(on_device, ny, nz),
        mesh=mesh,
        in_specs=(P("wide", None, None), P(None, "batch"), P(), P(), P()),
        out_specs=P(None, "wide", "batch", None),
        check_vma=False,
    )
```
